32 devices in a mesh: dp: 8 (over y, x, core), inner: 4 (over z).
Axes of the slice: x: 2, y: 2, z: 4, core: 2. Of those that a mesh axis runs over, the one named last changes fastest.
Arguments:
- tokens: bfloat16 [32, 1024, 768], P(('dp', 'inner')), may hold values from -6 to 6
- lengths: int32 [32], P(('dp', 'inner')), may hold values from 512 to 1024, as said below
- cotangent: bfloat16 [32, 1024, 768], P(('dp', 'inner')), may hold values from -6 to 6
- norm1_gain: bfloat16 [768], P(('dp', 'inner')), may hold values from 0.5 to 1.5
- norm1_bias: bfloat16 [768], P(('dp', 'inner')), may hold values from -1.5 to 1.5
- attn_in: bfloat16 [768, 2304], P(('dp', 'inner')), may hold values from -0.21875 to 0.21875
- attn_bias: bfloat16 [1536], P(('dp', 'inner')), may hold values from -2.5 to 2.5
- attn_out: bfloat16 [768, 768], P(('dp', 'inner')), may hold values from -1.75 to 1.75
- out_bias: bfloat16 [768], P(('dp', 'inner')), may hold values from -1.5 to 1.5
- norm2_gain: bfloat16 [768], P(('dp', 'inner')), may hold values from 0.5 to 1.5
- norm2_bias: bfloat16 [768], P(('dp', 'inner')), may hold values from -1.5 to 1.5
- mlp_up: bfloat16 [768, 3072], P(('dp', 'inner')), may hold values from -0.21875 to 0.21875
- up_bias: bfloat16 [3072], P(('dp', 'inner')), may hold values from -2.5 to 2.5
- mlp_down: bfloat16 [3072, 768], P(('dp', 'inner')), may hold values from -0.21875 to 0.21875
- down_bias: bfloat16 [768], P(('dp', 'inner')), may hold values from -1.5 to 1.5
Outputs:
- output: bfloat16 [32, 1024, 768], P(('dp', 'inner'))
- tokens_grad: bfloat16 [32, 1024, 768], P(('dp', 'inner'))
- norm1_gain_grad: float32 [768], P(('dp', 'inner'))
- norm1_bias_grad: float32 [768], P(('dp', 'inner'))
- attn_in_grad: float32 [768, 2304], P(('dp', 'inner'))
- attn_bias_grad: float32 [1536], P(('dp', 'inner'))
- attn_out_grad: float32 [768, 768], P(('dp', 'inner'))
- out_bias_grad: float32 [768], P(('dp', 'inner'))
- norm2_gain_grad: float32 [768], P(('dp', 'inner'))
- norm2_bias_grad: float32 [768], P(('dp', 'inner'))
- mlp_up_grad: float32 [768, 3072], P(('dp', 'inner'))
- up_bias_grad: float32 [3072], P(('dp', 'inner'))
- mlp_down_grad: float32 [3072, 768], P(('dp', 'inner'))
- down_bias_grad: float32 [768], P(('dp', 'inner'))
The draws below stay inside these ranges and needn't reach their ends.
Inputs may be any that keep to these rules, and one draw needn't show every extreme that they name: `lengths`: each length is 1024 or 512, and exactly half of the sequences have each.
All inputs are finite; a program needn't handle non-finite values.
Results may differ from the reference program's by a relative error of at most 0.011.
Values may be sent and summed in bfloat16 or wider, within the bound.
No kernel may reach another device: no remote copies, remote signals or barrier semaphores. Data moves between devices by JAX's collectives and lax.ppermute only.
A program may use at most 256 MiB of HBM per device.

```python
import jax
import jax.numpy as jnp
from jax import lax

D = 768
FF = 3072
TOK_DEV = 1024
SEQS = 32


def draw_lengths(key, part):
    order = jax.random.permutation(key, SEQS)
    return jnp.where(order < SEQS // 2, TOK_DEV, TOK_DEV // 2).astype(jnp.int32)


def block_levels(stream_key, dims, pieces, smallest, high):
    def one(axis_at, blocks):
        heights = jax.random.uniform(jax.random.fold_in(jax.random.fold_in(stream_key, 6), axis_at), (blocks,), jnp.float32, smallest / len(pieces), high / len(pieces))
        return jnp.repeat(jnp.exp(heights), dims[axis_at] // blocks).reshape((-1,) + (1,) * (len(dims) - axis_at - 1))

    level = one(*pieces[0])
    for cut in pieces[1:]:
        level = level * one(*cut)
    return level


def noise(stream_key, shape, scale, bound, pieces=(), kind=jnp.bfloat16):
    entries = scale * jax.random.normal(stream_key, shape, jnp.float32)
    if pieces:
        entries = entries * block_levels(stream_key, shape, pieces, -0.22, 0.18)
    return jnp.clip(entries, -bound, bound).astype(kind)


def setup_inputs(seed: int = 0) -> dict:
    arg_keys = jax.random.split(jax.random.key(seed), 16)
    tokens = noise(arg_keys[0], (SEQS, TOK_DEV, D), 1.0, 6.0, ((0, 32),))
    lengths = draw_lengths(jax.random.fold_in(arg_keys[15], 71), 0)
    cotangent = noise(arg_keys[2], (SEQS, TOK_DEV, D), 1.0, 6.0, ((0, 32),))
    norm1_gain = jnp.clip(1.0 + 0.1 * jax.random.normal(arg_keys[3], (D,), jnp.float32), 0.5, 1.5).astype(jnp.bfloat16)
    norm1_bias = noise(arg_keys[4], (D,), 0.3, 1.5, ((0, 32),))
    attn_in = noise(arg_keys[5], (D, 3 * D), D ** -0.5, 0.21875, ((0, 32),))
    attn_bias = noise(arg_keys[6], (2 * D,), 0.5, 2.5, ((0, 32),))
    attn_out = noise(arg_keys[7], (D, D), (D // 64) ** -0.5, 1.75, ((0, 32),))
    out_bias = noise(arg_keys[8], (D,), 0.3, 1.5, ((0, 32),))
    norm2_gain = jnp.clip(1.0 + 0.1 * jax.random.normal(arg_keys[9], (D,), jnp.float32), 0.5, 1.5).astype(jnp.bfloat16)
    norm2_bias = noise(arg_keys[10], (D,), 0.3, 1.5, ((0, 32),))
    mlp_up = noise(arg_keys[11], (D, FF), D ** -0.5, 0.21875, ((0, 32),))
    up_bias = noise(arg_keys[12], (FF,), 0.5, 2.5, ((0, 32),))
    mlp_down = noise(arg_keys[13], (FF, D), (FF // 4) ** -0.5, 0.21875, ((0, 32),))
    down_bias = noise(arg_keys[14], (D,), 0.3, 1.5, ((0, 32),))
    return dict(tokens=tokens, lengths=lengths, cotangent=cotangent, norm1_gain=norm1_gain, norm1_bias=norm1_bias, attn_in=attn_in, attn_bias=attn_bias, attn_out=attn_out, out_bias=out_bias, norm2_gain=norm2_gain, norm2_bias=norm2_bias, mlp_up=mlp_up, up_bias=up_bias, mlp_down=mlp_down, down_bias=down_bias)


@jax.custom_vjp
def low(v):
    return lax.optimization_barrier(v.astype(jnp.bfloat16)).astype(jnp.float32)

@jax.custom_vjp
def low_back(v):
    return v

def low_keep(v):
    return (low(v), None)

def low_pass(kept, grad):
    return (grad,)

def back_keep(v):
    return (v, None)

def back_low(kept, grad):
    return (low(grad),)
low.defvjp(low_keep, low_pass)
low_back.defvjp(back_keep, back_low)
EPSILON = 1e-05
SCALE = 0.125
MASKED = -1000000000.0

def norm_rows(values, gain, shift):
    centre = values - lax.optimization_barrier(jnp.mean(values, axis=-1, keepdims=True))
    spread = lax.optimization_barrier(jnp.mean(centre * centre, axis=-1, keepdims=True))
    return centre * lax.rsqrt(spread + EPSILON) * gain + shift

def gelu_tanh(values):
    return 0.5 * values * (1.0 + jnp.tanh(0.7978845608028654 * (values + 0.044715 * values * values * values)))

def matmul(left, right):
    return jnp.dot(left, right, precision=lax.Precision.HIGHEST)

def layer(inputs, params, count):
    gain_one, shift_one, w_in, bias_in, w_out, bias_out, gain_two, shift_two, w_up, bias_up, w_down, bias_down = params
    rows = inputs.shape[0]
    width = inputs.shape[1]
    heads = width // 64
    normed1 = low(norm_rows(inputs, gain_one, shift_one))
    zero_bias = jnp.zeros((width,), inputs.dtype)
    full_bias = jnp.concatenate([bias_in[:width], zero_bias, bias_in[width:]])
    qkv = low_back(low(matmul(normed1, w_in) + full_bias))
    queries = qkv[:, :width].reshape(rows, heads, 64)
    key_rows = qkv[:, width:2 * width].reshape(rows, heads, 64)
    value_rows = qkv[:, 2 * width:].reshape(rows, heads, 64)
    scores = low_back(SCALE * jnp.einsum('qhd,khd->hqk', queries, key_rows, precision=lax.Precision.HIGHEST))
    places = jnp.arange(rows, dtype=jnp.int32)
    allowed = places[None, :] <= places[:, None]
    scores = jnp.where(allowed[None], scores, MASKED)
    top_score = lax.optimization_barrier(jnp.max(scores, axis=-1, keepdims=True))
    expo = jnp.exp(scores - top_score)
    probs = expo / lax.optimization_barrier(jnp.sum(expo, axis=-1, keepdims=True))
    mixed = jnp.einsum('hqk,khd->qhd', low(probs), value_rows, precision=lax.Precision.HIGHEST).reshape(rows, width)
    live_rows = (places < count).astype(inputs.dtype)[:, None]
    mixed = low_back(low(mixed * live_rows))
    attended = low_back(matmul(mixed, w_out) + bias_out)
    resid = inputs + attended
    normed2 = low(norm_rows(resid, gain_two, shift_two))
    hidden = low_back(matmul(normed2, w_up) + bias_up)
    activated = low(gelu_tanh(hidden))
    branch = low_back(matmul(activated, w_down) + bias_down)
    return resid + branch

def reference(tokens, lengths, cotangent, norm1_gain, norm1_bias, attn_in, attn_bias, attn_out, out_bias, norm2_gain, norm2_bias, mlp_up, up_bias, mlp_down, down_bias):
    params = tuple((param.astype(jnp.float32) for param in (norm1_gain, norm1_bias, attn_in, attn_bias, attn_out, out_bias, norm2_gain, norm2_bias, mlp_up, up_bias, mlp_down, down_bias)))

    def one_sequence(totals, item):
        inputs, grads_in, count = item

        def apply_layer(values, weights):
            return layer(values, weights, count)
        result, pull = jax.vjp(apply_layer, inputs, params)
        input_grad, param_grads = pull(grads_in)
        totals = jax.tree.map(lambda total, grad: total + grad, totals, param_grads)
        return (totals, (result, input_grad))
    starts = jax.tree.map(jnp.zeros_like, params)
    totals, (results, input_grads) = lax.scan(one_sequence, starts, (tokens.astype(jnp.float32), cotangent.astype(jnp.float32), lengths))
    return (results.astype(jnp.bfloat16), input_grads.astype(jnp.bfloat16), totals[0], totals[1], totals[2], totals[3], totals[4], totals[5], totals[6], totals[7], totals[8], totals[9], totals[10], totals[11])
```

```python
import functools

import jax
import jax.numpy as jnp
from jax import lax
from jax.experimental import pallas as pl
from jax.experimental.pallas import tpu as pltpu
from jax.sharding import PartitionSpec as P

EPSILON = 1e-05
SCALE = 0.125
MASKED = -1000000000.0
AXES = ("dp", "inner")
HEAD = 64
PAIR = 2 * HEAD


def norm_stats(values):
    centre = values - jnp.mean(values, axis=-1, keepdims=True)
    spread = jnp.mean(centre * centre, axis=-1, keepdims=True)
    inverse = lax.rsqrt(spread + EPSILON)
    return centre * inverse, inverse


def norm_back(grad, xhat, inverse, gain):
    scaled = grad * gain
    first = jnp.mean(scaled, axis=-1, keepdims=True)
    second = jnp.mean(scaled * xhat, axis=-1, keepdims=True)
    return inverse * (scaled - first - xhat * second)


def gelu_both(values):
    inner = 0.7978845608028654 * (values + 0.044715 * values * values * values)
    bent = jnp.tanh(inner)
    half = 0.5 * (1.0 + bent)
    slope = half + 0.5 * values * (1.0 - bent * bent) * (
        0.7978845608028654 * (1.0 + 3.0 * 0.044715 * values * values)
    )
    return values * half, slope


def matmul(left, right):
    return jnp.dot(left, right, preferred_element_type=jnp.float32)


def matmul_tr(left, right):
    return lax.dot_general(
        left, right, (((1,), (1,)), ((), ())), preferred_element_type=jnp.float32
    )


def tr_matmul(left, right):
    return lax.dot_general(
        left, right, (((0,), (0,)), ((), ())), preferred_element_type=jnp.float32
    )


class Net:
    def __init__(self, dp, inner):
        self.count = dp * inner
        self.inner = inner
        self.rest = dp // 2
        self.inner_bits = [1 << b for b in range(inner.bit_length() - 1)]
        self.rest_bits = [1 << b for b in range(self.rest.bit_length() - 1)]
        place = lax.axis_index("dp")
        self.at_inner = lax.axis_index("inner")
        self.at_core = place % 2
        self.at_rest = place // 2

    def swap(self, value, mask):
        return lax.ppermute(value, AXES, [(i, i ^ mask) for i in range(self.count)])

    def swap_inner(self, value, bit):
        return self.swap(value, bit)

    def swap_core(self, value):
        return self.swap(value, self.inner)

    def swap_rest(self, value, bit):
        return self.swap(value, bit * self.inner * 2)

    def order(self, color):
        return self.rest_bits if color == 0 else self.rest_bits[::-1]

    def slot(self, rel, color):
        out = 0
        for at, bit in enumerate(self.order(color)):
            out = out + (((rel // bit) % 2) << at)
        return out

    def gather_inner(self, shards):
        rows = [shard[None] for shard in shards]
        for bit in self.inner_bits[::-1]:
            rows = [jnp.concatenate([x, self.swap_inner(x, bit)], axis=0) for x in rows]
        places = []
        for z in range(self.inner):
            rel = self.at_inner ^ z
            flat = 0
            for at, bit in enumerate(self.inner_bits[::-1]):
                flat = flat + (((rel // bit) % 2) << at)
            places.append(flat)
        return [
            jnp.concatenate(
                [lax.dynamic_index_in_dim(x, flat, 0, keepdims=False) for flat in places], axis=0
            )[None]
            for x in rows
        ]

    def gather_rest(self, groups, colors):
        for step in range(len(self.rest_bits)):
            groups = [
                jnp.concatenate([x, self.swap_rest(x, self.order(c)[step])], axis=0)
                for x, c in zip(groups, colors)
            ]
        return groups

    def gather(self, shards, colors):
        groups = self.gather_rest(self.gather_inner(shards), colors)
        return [(x, self.swap_core(x)) for x in groups]

    def assemble(self, pair, color):
        own, other = pair
        both = jnp.concatenate([own, other], axis=0)
        blocks = []
        for rest in range(self.rest):
            for core in range(2):
                flat = (self.at_core ^ core) * self.rest + self.slot(self.at_rest ^ rest, color)
                blocks.append(lax.dynamic_index_in_dim(both, flat, 0, keepdims=False))
        return jnp.concatenate(blocks, axis=0)

    def split(self, grad, color):
        rows, cols = grad.shape
        view = grad.astype(jnp.bfloat16).reshape(self.rest, 2, rows // (2 * self.rest), cols)
        halves = []
        for core in (self.at_core, 1 - self.at_core):
            half = lax.dynamic_index_in_dim(view, core, 1, keepdims=False)
            blocks = [None] * self.rest
            for rel in range(self.rest):
                blocks[self.slot(rel, color)] = lax.dynamic_index_in_dim(
                    half, self.at_rest ^ rel, 0, keepdims=True
                )
            halves.append(jnp.concatenate(blocks, axis=0))
        return halves

    def scatter(self, halves, colors):
        def add(a, b):
            return (a.astype(jnp.float32) + b.astype(jnp.float32)).astype(jnp.bfloat16)

        sums = []
        for keep, send in halves:
            recv = self.swap_core(send)
            n = keep.shape[0] // 2
            sums.append((add(keep[:n], recv[:n]), add(keep[n:], recv[n:])))
        steps = len(self.rest_bits)
        for step in range(steps):
            following = []
            for (keep, send), c in zip(sums, colors):
                recv = self.swap_rest(send, self.order(c)[steps - 1 - step])
                if step < steps - 1:
                    n = keep.shape[0] // 2
                    following.append((add(keep[:n], recv[:n]), add(keep[n:], recv[n:])))
                else:
                    following.append(add(keep, recv))
            sums = following
        out = []
        for x in sums:
            rows = x.shape[1] // self.inner
            view = x.reshape(self.inner, rows, x.shape[2])
            total = lax.dynamic_index_in_dim(view, self.at_inner, 0, keepdims=False).astype(
                jnp.float32
            )
            for mask in range(1, self.inner):
                send = lax.dynamic_index_in_dim(view, self.at_inner ^ mask, 0, keepdims=False)
                total = total + self.swap(send, mask).astype(jnp.float32)
            out.append(total)
        return out


def attention_forward_kernel(step, count_ref, q_ref, k_ref, v_ref, mixed_ref, log_ref):
    rows = q_ref.shape[0]
    count = count_ref[0]
    for head in range(2):
        cols = slice(head * HEAD, (head + 1) * HEAD)
        turned = jnp.transpose(v_ref[:, cols].astype(jnp.float32)).astype(jnp.bfloat16)
        for start in range(0, rows, step):
            end = start + step

            def block():
                query = q_ref[start:end, cols] * jnp.bfloat16(SCALE)
                scores = matmul_tr(k_ref[0:end, cols], query)
                keys_at = lax.broadcasted_iota(jnp.int32, (step, step), 0)
                rows_at = lax.broadcasted_iota(jnp.int32, (step, step), 1)
                last = jnp.where(keys_at <= rows_at, scores[start:end], MASKED)
                scores = jnp.concatenate([scores[:start], last], axis=0) if start else last
                top = jnp.max(scores, axis=0, keepdims=True)
                expo = jnp.exp(scores - top)
                total = jnp.sum(expo, axis=0, keepdims=True)
                out = matmul(turned[:, 0:end], expo.astype(jnp.bfloat16)) / total
                live = lax.broadcasted_iota(jnp.int32, (1, step), 1) + start < count
                out = jnp.where(live, out, 0.0)
                mixed_ref[start:end, cols] = jnp.transpose(out).astype(jnp.bfloat16)
                log_ref[0, head : head + 1, start:end] = top + jnp.log(total)

            def empty():
                mixed_ref[start:end, cols] = jnp.zeros((step, HEAD), jnp.bfloat16)
                log_ref[0, head : head + 1, start:end] = jnp.zeros((1, step), jnp.float32)

            if start == 0:
                block()
            else:
                pl.when(start < count)(block)
                pl.when(start >= count)(empty)


def attention_forward(qkv, count, first, pairs):
    rows, wide = qkv.shape
    total = wide // (3 * PAIR)
    step = min(256, rows)
    return pl.pallas_call(
        functools.partial(attention_forward_kernel, step),
        grid_spec=pltpu.PrefetchScalarGridSpec(
            num_scalar_prefetch=1,
            grid=(pairs,),
            in_specs=[
                pl.BlockSpec((rows, PAIR), lambda i, n: (0, first + i)),
                pl.BlockSpec((rows, PAIR), lambda i, n: (0, total + first + i)),
                pl.BlockSpec((rows, PAIR), lambda i, n: (0, 2 * total + first + i)),
            ],
            out_specs=[
                pl.BlockSpec((rows, PAIR), lambda i, n: (0, i)),
                pl.BlockSpec((1, 2, rows), lambda i, n: (i, 0, 0)),
            ],
        ),
        out_shape=[
            jax.ShapeDtypeStruct((rows, pairs * PAIR), jnp.bfloat16),
            jax.ShapeDtypeStruct((pairs, 2, rows), jnp.float32),
        ],
        cost_estimate=pl.CostEstimate(
            flops=pairs * 2 * rows * rows * 256 * 2,
            bytes_accessed=pairs * rows * PAIR * 8,
            transcendentals=pairs * rows * rows,
        ),
        name="attention_forward",
    )(count, qkv, qkv, qkv)


def attention_backward_kernel(
    step,
    count_ref,
    q_ref,
    k_ref,
    v_ref,
    mixed_ref,
    grad_ref,
    log_ref,
    dq_ref,
    dk_ref,
    dv_ref,
    dk_acc,
    dv_acc,
):
    rows = q_ref.shape[0]
    count = count_ref[0]
    prod = grad_ref[...].astype(jnp.float32) * mixed_ref[...].astype(jnp.float32)
    prod = jnp.transpose(prod)
    for head in range(2):
        cols = slice(head * HEAD, (head + 1) * HEAD)
        inner = jnp.sum(prod[cols], axis=0, keepdims=True)
        turned = jnp.transpose(k_ref[:, cols].astype(jnp.float32)).astype(jnp.bfloat16)
        dk_acc[...] = jnp.zeros_like(dk_acc)
        dv_acc[...] = jnp.zeros_like(dv_acc)
        for start in range(0, rows, step):
            end = start + step

            def block():
                query = q_ref[start:end, cols] * jnp.bfloat16(SCALE)
                grad = grad_ref[start:end, cols]
                scores = matmul_tr(k_ref[0:end, cols], query)
                probs = jnp.exp(scores - log_ref[0, head : head + 1, start:end])
                keys_at = lax.broadcasted_iota(jnp.int32, (step, step), 0)
                rows_at = lax.broadcasted_iota(jnp.int32, (step, step), 1)
                last = jnp.where(keys_at <= rows_at, probs[start:end], 0.0)
                probs = jnp.concatenate([probs[:start], last], axis=0) if start else last
                dv_acc[0:end] += matmul(probs.astype(jnp.bfloat16), grad)
                dprobs = matmul_tr(v_ref[0:end, cols], grad)
                dscores = (probs * (dprobs - inner[:, start:end])).astype(jnp.bfloat16)
                dk_acc[0:end] += matmul(dscores, query)
                dq = matmul(turned[:, 0:end], dscores) * SCALE
                dq_ref[start:end, cols] = jnp.transpose(dq).astype(jnp.bfloat16)

            def empty():
                dq_ref[start:end, cols] = jnp.zeros((step, HEAD), jnp.bfloat16)

            if start == 0:
                block()
            else:
                pl.when(start < count)(block)
                pl.when(start >= count)(empty)
        dk_ref[:, cols] = dk_acc[...].astype(jnp.bfloat16)
        dv_ref[:, cols] = dv_acc[...].astype(jnp.bfloat16)


def attention_backward(qkv, mixed, grad, logs, count, first, pairs):
    rows, wide = qkv.shape
    total = wide // (3 * PAIR)
    step = min(256, rows)
    part = jax.ShapeDtypeStruct((rows, pairs * PAIR), jnp.bfloat16)
    return pl.pallas_call(
        functools.partial(attention_backward_kernel, step),
        grid_spec=pltpu.PrefetchScalarGridSpec(
            num_scalar_prefetch=1,
            grid=(pairs,),
            in_specs=[
                pl.BlockSpec((rows, PAIR), lambda i, n: (0, first + i)),
                pl.BlockSpec((rows, PAIR), lambda i, n: (0, total + first + i)),
                pl.BlockSpec((rows, PAIR), lambda i, n: (0, 2 * total + first + i)),
                pl.BlockSpec((rows, PAIR), lambda i, n: (0, i)),
                pl.BlockSpec((rows, PAIR), lambda i, n: (0, first + i)),
                pl.BlockSpec((1, 2, rows), lambda i, n: (i, 0, 0)),
            ],
            out_specs=[pl.BlockSpec((rows, PAIR), lambda i, n: (0, i))] * 3,
            scratch_shapes=[pltpu.VMEM((rows, HEAD), jnp.float32)] * 2,
        ),
        out_shape=[part] * 3,
        cost_estimate=pl.CostEstimate(
            flops=pairs * 2 * rows * rows * 256 * 5,
            bytes_accessed=pairs * rows * PAIR * 16,
            transcendentals=pairs * rows * rows,
        ),
        name="attention_backward",
    )(count, qkv, qkv, qkv, mixed, grad, logs)


def local(
    dp,
    inner,
    tokens,
    lengths,
    cotangent,
    norm1_gain,
    norm1_bias,
    attn_in,
    attn_bias,
    attn_out,
    out_bias,
    norm2_gain,
    norm2_bias,
    mlp_up,
    up_bias,
    mlp_down,
    down_bias,
):
    net = Net(dp, inner)
    n = net.count
    tok = tokens[0]
    grad_out = cotangent[0]
    rows, width = tok.shape
    wide = mlp_up.shape[1]
    r = attn_in.shape[0]
    places = jnp.arange(rows, dtype=jnp.int32)
    count = lengths[0]

    small = jnp.concatenate(
        [norm1_gain, norm1_bias, attn_bias, out_bias, norm2_gain, norm2_bias, up_bias, down_bias]
    )
    sizes = [r, r, 2 * r, r, r, r, up_bias.shape[0], r]
    padded = -(-small.shape[0] // 128) * 128
    small = jnp.pad(small, (0, padded - small.shape[0]))[None]

    half = 3 * width // 2
    in_a, in_b, small_all = net.gather(
        [attn_in[:, :half], attn_in[:, half:], small], [0, 1, 0]
    )
    w_in = jnp.concatenate([net.assemble(in_a, 0), net.assemble(in_b, 1)], axis=1)
    small_all = net.assemble(small_all, 0)
    pieces = []
    at = 0
    for size in sizes:
        pieces.append(small_all[:, at : at + size].reshape(-1).astype(jnp.float32))
        at += size
    gain_one, shift_one, bias_in, bias_out, gain_two, shift_two, bias_up, bias_down = pieces

    out_a, out_b, down, up = net.gather(
        [attn_out[:, : width // 2], attn_out[:, width // 2 :], mlp_down, mlp_up], [0, 1, 0, 1]
    )
    w_out = jnp.concatenate([net.assemble(out_a, 0), net.assemble(out_b, 1)], axis=1)
    w_up = net.assemble(up, 1)
    w_down = net.assemble(down, 0)

    inputs = tok.astype(jnp.float32)
    xhat1, inverse1 = norm_stats(inputs)
    normed1 = (xhat1 * gain_one + shift_one).astype(jnp.bfloat16)
    full_bias = jnp.concatenate([bias_in[:width], jnp.zeros((width,), jnp.float32), bias_in[width:]])
    qkv = (matmul(normed1, w_in) + full_bias).astype(jnp.bfloat16)
    pairs = width // PAIR
    groups = 3 if pairs % 3 == 0 else 1
    each = pairs // groups
    mixed_parts = []
    log_parts = []
    for g in range(groups):
        part, logs = attention_forward(qkv, lengths, g * each, each)
        mixed_parts.append(part)
        log_parts.append(logs)
    mixed = jnp.concatenate(mixed_parts, axis=1)
    resid = inputs + matmul(mixed, w_out) + bias_out
    xhat2, inverse2 = norm_stats(resid)
    normed2 = (xhat2 * gain_two + shift_two).astype(jnp.bfloat16)
    hidden = matmul(normed2, w_up) + bias_up
    act_float, slope = gelu_both(hidden)
    activated = act_float.astype(jnp.bfloat16)
    output = (resid + matmul(activated, w_down) + bias_down).astype(jnp.bfloat16)

    grad_float = grad_out.astype(jnp.float32)
    down_grad = tr_matmul(activated, grad_out)
    down_bias_grad = jnp.sum(grad_float, axis=0)
    hidden_grad = (matmul_tr(grad_out, w_down) * slope).astype(jnp.bfloat16)
    up_grad = tr_matmul(normed2, hidden_grad)
    up_bias_grad = jnp.sum(hidden_grad.astype(jnp.float32), axis=0)
    down_sum, up_sum = net.scatter(
        [net.split(down_grad, 0), net.split(up_grad, 1)], [0, 1]
    )
    normed2_grad = matmul_tr(hidden_grad, w_up)
    gain_two_grad = jnp.sum(normed2_grad * xhat2, axis=0)
    shift_two_grad = jnp.sum(normed2_grad, axis=0)
    resid_grad = grad_float + norm_back(normed2_grad, xhat2, inverse2, gain_two)
    resid_low = resid_grad.astype(jnp.bfloat16)
    out_grad = tr_matmul(mixed, resid_low)
    out_bias_grad = jnp.sum(resid_low.astype(jnp.float32), axis=0)
    live = (places < count).astype(jnp.float32)[:, None]
    mixed_grad = (matmul_tr(resid_low, w_out) * live).astype(jnp.bfloat16)
    dq, dk, dv = [], [], []
    for g in range(groups):
        parts = attention_backward(
            qkv, mixed_parts[g], mixed_grad, log_parts[g], lengths, g * each, each
        )
        dq.append(parts[0])
        dk.append(parts[1])
        dv.append(parts[2])
    qkv_grad = jnp.concatenate(dq + dk + dv, axis=1)
    in_grad = tr_matmul(normed1, qkv_grad)
    qkv_sums = jnp.sum(qkv_grad.astype(jnp.float32), axis=0)
    bias_in_grad = jnp.concatenate([qkv_sums[:width], qkv_sums[2 * width :]])
    normed1_grad = matmul_tr(qkv_grad, w_in)
    gain_one_grad = jnp.sum(normed1_grad * xhat1, axis=0)
    shift_one_grad = jnp.sum(normed1_grad, axis=0)
    tokens_grad = (resid_grad + norm_back(normed1_grad, xhat1, inverse1, gain_one)).astype(
        jnp.bfloat16
    )
    small_grads = [
        gain_one_grad,
        shift_one_grad,
        bias_in_grad,
        out_bias_grad,
        gain_two_grad,
        shift_two_grad,
        up_bias_grad,
        down_bias_grad,
    ]
    small_grad = jnp.concatenate([g.reshape(n, -1) for g in small_grads], axis=1)
    small_grad = jnp.pad(small_grad, ((0, 0), (0, padded - small_grad.shape[1])))
    in_sum_a, in_sum_b, out_sum, small_sum = net.scatter(
        [
            net.split(in_grad[:, :half], 0),
            net.split(in_grad[:, half:], 1),
            net.split(out_grad, 0),
            net.split(small_grad, 1),
        ],
        [0, 1, 0, 1],
    )
    in_sum = jnp.concatenate([in_sum_a, in_sum_b], axis=1)
    outs = []
    at = 0
    for size in sizes:
        outs.append(small_sum[0, at : at + size])
        at += size
    return (
        output[None],
        tokens_grad[None],
        outs[0],
        outs[1],
        in_sum,
        outs[2],
        out_sum,
        outs[3],
        outs[4],
        outs[5],
        up_sum,
        outs[6],
        down_sum,
        outs[7],
    )


def solution(mesh):
    rows = P(AXES)
    flat = P(AXES, None)
    deep = P(AXES, None, None)
    return jax.shard_map(
        functools.partial(local, mesh.shape["dp"], mesh.shape["inner"]),
        mesh=mesh,
        in_specs=(
            deep,
            rows,
            deep,
            rows,
            rows,
            flat,
            rows,
            flat,
            rows,
            rows,
            rows,
            flat,
            rows,
            flat,
            rows,
        ),
        out_specs=(
            deep,
            deep,
            rows,
            rows,
            flat,
            rows,
            flat,
            rows,
            rows,
            rows,
            flat,
            rows,
            flat,
            rows,
        ),
        check_vma=False,
    )
```
